768 devices in a mesh: lst: 32 (over y, x), freq: 24 (over z, core).
Axes of the slice: x: 4, y: 8, z: 12, core: 2. Of those that a mesh axis runs over, the one named last changes fastest.
Arguments:
- visibilities: bfloat16 [2, 768, 288, 768], P(None, ('lst', 'freq')), may hold values from -6 to 6
- model_vis: bfloat16 [2, 768, 288, 768], P(None, ('lst', 'freq')), may hold values from -6 to 6
- antenna_gains: bfloat16 [2, 768, 256, 768], P(None, ('lst', 'freq')), may hold values from -6 to 6
- baseline_antenna_index: int32 [2, 288], replicated, may hold values from 0 to 255, as said below
- flag_tiles: int32 [768, 288, 6], P(('lst', 'freq')), may hold values 0 or 1
- kernel: float32 [5], replicated, may hold values from 0.1 to 0.3
Outputs:
- smoothed_step: bfloat16 [2, 768, 256, 768], P(None, 'lst', None, 'freq')
The draws below stay inside these ranges and needn't reach their ends.
Inputs may be any that keep to these rules, and one draw needn't show every extreme that they name: `baseline_antenna_index`: in each column the two antennas differ; every antenna appears in the first row.
All inputs are finite; a program needn't handle non-finite values. No bound on the sum of `flag_tiles` on one device may be relied on, other than what follows from the above.
Results may differ from the reference program's by a relative error of at most 0.0053.
Values may be sent and summed in bfloat16 or wider, within the bound.
A program may use at most 32 MiB of HBM per device.

```python
import jax
import jax.numpy as jnp
from jax import lax

ANTENNA_COUNT = 256
CH = 768
TILE = 128
W = 2
BASELINE_COUNT = 288
TIMES = 768


def draw_baseline_antenna_index(key, part):
    key_order, key_offset = jax.random.split(key)
    permuted_rows = jax.random.permutation(key_order, ANTENNA_COUNT)
    leading_antenna = permuted_rows[jnp.arange(BASELINE_COUNT) % ANTENNA_COUNT]
    index_shift = jax.random.randint(key_offset, (BASELINE_COUNT,), 1, ANTENNA_COUNT)
    trailing_antenna = (leading_antenna + index_shift) % ANTENNA_COUNT
    return jnp.stack([leading_antenna, trailing_antenna]).astype(jnp.int32)


def with_ends(values, own_key, low, high):
    dims = values.shape
    place = [jax.random.randint(jax.random.fold_in(own_key, axis), (), 0, dims[axis]) for axis in range(len(dims))]
    values = values.at[tuple(place)].set(low)
    longest = dims.index(max(dims))
    place[longest] = (place[longest] + 1) % dims[longest]
    return values.at[tuple(place)].set(high)


def levels(rng, dims, cuts, smallest, top_value):
    gain = 1.0
    for axis_at, shards_of in cuts:
        steps = jax.random.uniform(jax.random.fold_in(jax.random.fold_in(rng, 6), axis_at), (shards_of,), jnp.float32, smallest / len(cuts), top_value / len(cuts))
        gain = gain * jnp.repeat(jnp.exp(steps), dims[axis_at] // shards_of).reshape((-1,) + (1,) * (len(dims) - 1 - axis_at))
    return gain


def centred(key, dims, spread, limit, cuts=(), held_as=jnp.bfloat16):
    gain = levels(key, dims, cuts, -0.22, 0.18) if cuts else 1.0
    values = jax.random.normal(key, dims, jnp.float32) * spread * gain
    return jnp.minimum(jnp.maximum(values, -limit), limit).astype(held_as)


def setup_inputs(seed: int = 0) -> dict:
    key_list = jax.random.split(jax.random.key(seed), 7)
    return {
        "visibilities": centred(key_list[0], (2, TIMES, BASELINE_COUNT, CH), 1.0, 6.0, ((1, 768),)),
        "model_vis": centred(key_list[1], (2, TIMES, BASELINE_COUNT, CH), 1.0, 6.0, ((1, 768),)),
        "antenna_gains": centred(key_list[2], (2, TIMES, ANTENNA_COUNT, CH), 1.0, 6.0, ((1, 768),)),
        "baseline_antenna_index": draw_baseline_antenna_index(jax.random.fold_in(key_list[6], 71), 0),
        "flag_tiles": with_ends((jax.random.randint(key_list[4], (TIMES, BASELINE_COUNT, CH // TILE), 0, 4) < 3).astype(jnp.int32), jax.random.fold_in(key_list[4], 1), 0, 1),
        "kernel": jnp.clip(jax.random.uniform(key_list[5], (2 * W + 1,), jnp.float32, 0.1, 0.3), 0.1, 0.3),
    }


def baseline_terms(leading_gain, trailing_gain, data_row, model_row, weight):
    first_re, first_im = leading_gain[0], leading_gain[1]
    second_re, second_im = trailing_gain[0], trailing_gain[1]
    data_re, data_im = data_row[0], data_row[1]
    model_re, model_im = model_row[0], model_row[1]
    cross_re = first_re * second_re + first_im * second_im
    cross_im = first_im * second_re - first_re * second_im
    pred_re = cross_re * model_re - cross_im * model_im
    pred_im = cross_re * model_im + cross_im * model_re
    resid_re = weight * (data_re - pred_re)
    resid_im = weight * (data_im - pred_im)
    along_re = second_re * model_re + second_im * model_im
    along_im = second_im * model_re - second_re * model_im
    leading_term = jnp.stack([resid_re * along_re - resid_im * along_im, resid_re * along_im + resid_im * along_re])
    other_re = first_re * model_re - first_im * model_im
    other_im = first_re * model_im + first_im * model_re
    trailing_term = jnp.stack([resid_re * other_re + resid_im * other_im, resid_re * other_im - resid_im * other_re])
    return leading_term, trailing_term


def reference(visibilities, model_vis, antenna_gains, baseline_antenna_index, flag_tiles, kernel):
    leading_antenna = baseline_antenna_index[0]
    trailing_antenna = baseline_antenna_index[1]

    def one_time(inputs):
        data_row, model_row, gain_vector, flag_row = inputs
        leading_gain = gain_vector[:, leading_antenna, :].astype(jnp.float32)
        trailing_gain = gain_vector[:, trailing_antenna, :].astype(jnp.float32)
        flag_as_real = flag_row.astype(jnp.float32)
        weight = jnp.repeat(flag_as_real, TILE, axis=1)
        leading_term, trailing_term = baseline_terms(leading_gain, trailing_gain, data_row.astype(jnp.float32), model_row.astype(jnp.float32), weight)
        leading_term = lax.optimization_barrier(leading_term.astype(jnp.bfloat16)).astype(jnp.float32)
        trailing_term = lax.optimization_barrier(trailing_term.astype(jnp.bfloat16)).astype(jnp.float32)
        leading_sums = jax.ops.segment_sum(jnp.moveaxis(leading_term, 1, 0), leading_antenna, ANTENNA_COUNT)
        trailing_sums = jax.ops.segment_sum(jnp.moveaxis(trailing_term, 1, 0), trailing_antenna, ANTENNA_COUNT)
        antenna_sums = jnp.moveaxis(leading_sums + trailing_sums, 0, 1)
        baseline_counts = jax.ops.segment_sum(flag_as_real, leading_antenna, ANTENNA_COUNT) + jax.ops.segment_sum(flag_as_real, trailing_antenna, ANTENNA_COUNT)
        scale = 1.0 + jnp.repeat(baseline_counts, TILE, axis=1)
        return (antenna_sums / scale[None]).astype(jnp.bfloat16)

    partial_value = lax.map(one_time, (jnp.moveaxis(visibilities, 1, 0), jnp.moveaxis(model_vis, 1, 0), jnp.moveaxis(antenna_gains, 1, 0), flag_tiles))
    partial_value = jnp.moveaxis(partial_value, 0, 1)
    update = jnp.zeros(partial_value.shape, jnp.float32)
    for shift_index in range(2 * W + 1):
        update = update + kernel[shift_index] * jnp.roll(partial_value, W - shift_index, axis=1).astype(jnp.float32)
    return update.astype(jnp.bfloat16)
```

```python
import jax
import jax.numpy as jnp
from jax import lax
from jax.sharding import PartitionSpec as P


def extended(array, sides, width):
    for axis, dim in sides:
        size, length = (lax.axis_size(axis), array.shape[dim])
        up = [(i, (i + 1) % size) for i in range(size)]
        down = [(j, i) for i, j in up]
        last = lax.slice_in_dim(array, length - width, length, axis=dim)
        leading = lax.slice_in_dim(array, 0, width, axis=dim)
        before = lax.ppermute(last, axis, up)
        after = lax.ppermute(leading, axis, down)
        array = jnp.concatenate([before, array, after], axis=dim)
    return array


def baseline_terms(leading_gain, trailing_gain, data_row, model_row, weight):
    first_re, first_im = (leading_gain[0], leading_gain[1])
    second_re, second_im = (trailing_gain[0], trailing_gain[1])
    data_re, data_im = (data_row[0], data_row[1])
    model_re, model_im = (model_row[0], model_row[1])
    cross_re = first_re * second_re + first_im * second_im
    cross_im = first_im * second_re - first_re * second_im
    pred_re = cross_re * model_re - cross_im * model_im
    pred_im = cross_re * model_im + cross_im * model_re
    resid_re = weight * (data_re - pred_re)
    resid_im = weight * (data_im - pred_im)
    along_re = second_re * model_re + second_im * model_im
    along_im = second_im * model_re - second_re * model_im
    leading_term = jnp.stack(
        [resid_re * along_re - resid_im * along_im, resid_re * along_im + resid_im * along_re]
    )
    other_re = first_re * model_re - first_im * model_im
    other_im = first_re * model_im + first_im * model_re
    trailing_term = jnp.stack(
        [resid_re * other_re + resid_im * other_im, resid_re * other_im - resid_im * other_re]
    )
    return (leading_term, trailing_term)


def body(visibilities, model_vis, antenna_gains, baseline_antenna_index, flag_tiles, kernel):
    antenna_list = antenna_gains.shape[2]
    baseline_list = baseline_antenna_index.shape[1]
    tile_width = visibilities.shape[3] // flag_tiles.shape[2]
    segment_labels = lax.broadcasted_iota(jnp.int32, (baseline_list, antenna_list), 1)
    hot_first = (baseline_antenna_index[0][:, None] == segment_labels).astype(jnp.bfloat16)
    hot_second = (baseline_antenna_index[1][:, None] == segment_labels).astype(jnp.bfloat16)
    leading_gain = jnp.einsum(
        "ba,rtac->rtbc", hot_first, antenna_gains, preferred_element_type=jnp.float32
    )
    trailing_gain = jnp.einsum(
        "ba,rtac->rtbc", hot_second, antenna_gains, preferred_element_type=jnp.float32
    )
    weight = jnp.repeat(flag_tiles.astype(jnp.float32), tile_width, axis=2)
    leading_term, trailing_term = baseline_terms(
        leading_gain,
        trailing_gain,
        visibilities.astype(jnp.float32),
        model_vis.astype(jnp.float32),
        weight,
    )
    antenna_sums = jnp.einsum(
        "ba,rtbc->rtac",
        hot_first,
        leading_term.astype(jnp.bfloat16),
        preferred_element_type=jnp.float32,
    )
    antenna_sums = antenna_sums + jnp.einsum(
        "ba,rtbc->rtac",
        hot_second,
        trailing_term.astype(jnp.bfloat16),
        preferred_element_type=jnp.float32,
    )
    baseline_counts = jnp.einsum(
        "ba,tbk->tak",
        hot_first + hot_second,
        flag_tiles.astype(jnp.bfloat16),
        preferred_element_type=jnp.float32,
    )
    partial_value = (
        antenna_sums / (1.0 + jnp.repeat(baseline_counts, tile_width, axis=2))[None]
    ).astype(jnp.bfloat16)
    half_width = (kernel.shape[0] - 1) // 2
    received = lax.all_to_all(partial_value, "freq", split_axis=3, concat_axis=1, tiled=True)
    padded = extended(received, (("lst", 1),), half_width)
    row_count = padded.shape[1] - 2 * half_width
    update = jnp.zeros((padded.shape[0], row_count, padded.shape[2], padded.shape[3]), jnp.float32)
    for shift_index in range(2 * half_width + 1):
        update = update + kernel[shift_index] * padded[
            :, shift_index : shift_index + row_count
        ].astype(jnp.float32)
    return update.astype(jnp.bfloat16)


def solution(mesh):
    in_specs = (
        P(None, ("lst", "freq"), None, None),
        P(None, ("lst", "freq"), None, None),
        P(None, ("lst", "freq"), None, None),
        P(),
        P(("lst", "freq"), None, None),
        P(),
    )
    out_specs = P(None, "lst", None, "freq")
    return jax.shard_map(body, mesh=mesh, in_specs=in_specs, out_specs=out_specs, check_vma=False)
```

```python
import functools

import jax
import jax.numpy as jnp
from jax import lax
from jax.experimental import pallas as pl
from jax.experimental.pallas import tpu as pltpu
from jax.sharding import PartitionSpec as P

MESH = pl.DeviceIdType.MESH
LANES = 128
ROWS = 32
HALF = 2


def over_first(left, right):
    return lax.dot_general(
        left, right, (((0,), (0,)), ((), ())), preferred_element_type=jnp.float32
    )


def gradient_kernel(
    groups,
    blocks,
    vis_ref,
    model_ref,
    gain_ref,
    small_ref,
    kernel_ref,
    out_ref,
    data,
    model,
    gain,
    hot,
    inverse,
    weight,
    picked,
    terms,
    packed,
    bins,
    in_sem,
    send_sem,
    recv_sem,
    edge_send,
    edge_recv,
):
    tiles = data.shape[0]
    per_tile = groups // tiles
    width = LANES // per_tile
    count = data.shape[2]
    antennas = gain.shape[1]
    me = lax.axis_index("freq")
    block = lax.axis_index("lst")
    after = lax.rem(block + 1, blocks)
    before = lax.rem(block + blocks - 1, blocks)

    barrier = pltpu.get_barrier_semaphore()

    def greet(step, carry):
        peer = lax.rem(me + step, groups)
        pl.semaphore_signal(barrier, inc=1, device_id={"freq": peer}, device_id_type=MESH)
        return carry

    for peer in (before, after):
        pl.semaphore_signal(barrier, inc=1, device_id={"lst": peer}, device_id_type=MESH)
    lax.fori_loop(1, groups, greet, 0)

    def tile_of(i):
        turn = (1 - 2 * lax.rem(i, 2)) * ((i + 1) // 2)
        return lax.rem(me // per_tile + tiles // 2 + turn + tiles, tiles)

    def loads(i):
        lanes = pl.ds(pl.multiple_of(tile_of(i) * LANES, LANES), LANES)
        return [
            pltpu.make_async_copy(gain_ref.at[0, 0, :, lanes], gain.at[i, :, pl.ds(0, LANES)], in_sem.at[i, 0]),
            pltpu.make_async_copy(gain_ref.at[1, 0, :, lanes], gain.at[i, :, pl.ds(LANES, LANES)], in_sem.at[i, 1]),
            pltpu.make_async_copy(vis_ref.at[:, 0, :, lanes], data.at[i], in_sem.at[i, 2]),
            pltpu.make_async_copy(model_ref.at[:, 0, :, lanes], model.at[i], in_sem.at[i, 3]),
        ]

    def start_loads(i, carry):
        for copy in loads(i):
            copy.start()
        return carry

    lax.fori_loop(0, tiles, start_loads, 0)

    small = small_ref[...]
    row = lax.broadcasted_iota(jnp.int32, (small.shape[0], antennas), 0)
    antenna = lax.broadcasted_iota(jnp.int32, (count, antennas), 1).astype(jnp.float32)
    for which in range(2):
        label = over_first(small, (row == which).astype(jnp.bfloat16))
        hot[which * count : (which + 1) * count, :] = (label == antenna).astype(jnp.bfloat16)
    used = jnp.dot(
        small, hot[:count, :] + hot[count:, :], preferred_element_type=jnp.float32
    )
    inverse[...] = 1.0 / (1.0 + used)

    def compute(i):
        tile = tile_of(i)
        for copy in loads(i):
            copy.wait()
        picked[...] = jnp.dot(hot[...], gain[i], preferred_element_type=jnp.float32)
        weight[...] = over_first(small, (row[:, :LANES] == tile + 2).astype(jnp.bfloat16))
        for start in range(0, count, ROWS):
            here = slice(start, start + ROWS)
            there = slice(count + start, count + start + ROWS)
            first_re, first_im = picked[here, :LANES], picked[here, LANES:]
            second_re, second_im = picked[there, :LANES], picked[there, LANES:]
            data_re = data[i, 0, here, :].astype(jnp.float32)
            data_im = data[i, 1, here, :].astype(jnp.float32)
            model_re = model[i, 0, here, :].astype(jnp.float32)
            model_im = model[i, 1, here, :].astype(jnp.float32)
            flag = weight[here, :]
            cross_re = first_re * second_re + first_im * second_im
            cross_im = first_im * second_re - first_re * second_im
            pred_re = cross_re * model_re - cross_im * model_im
            pred_im = cross_re * model_im + cross_im * model_re
            resid_re = flag * (data_re - pred_re)
            resid_im = flag * (data_im - pred_im)
            along_re = second_re * model_re + second_im * model_im
            along_im = second_im * model_re - second_re * model_im
            terms[here, :LANES] = (resid_re * along_re - resid_im * along_im).astype(jnp.bfloat16)
            terms[here, LANES:] = (resid_re * along_im + resid_im * along_re).astype(jnp.bfloat16)
            other_re = first_re * model_re - first_im * model_im
            other_im = first_re * model_im + first_im * model_re
            terms[there, :LANES] = (resid_re * other_re + resid_im * other_im).astype(jnp.bfloat16)
            terms[there, LANES:] = (resid_re * other_im - resid_im * other_re).astype(jnp.bfloat16)
        sums = over_first(terms[...], hot[...])
        value = (sums * inverse[pl.ds(tile + 2, 1), :]).astype(jnp.bfloat16)
        for part in range(2):
            for j in range(per_tile):
                low = part * LANES + j * width
                packed[tile * per_tile + j, part] = value[low : low + width, :]

    def outgoing(peer):
        return pltpu.make_async_remote_copy(
            src_ref=packed.at[peer],
            dst_ref=bins.at[me + HALF],
            send_sem=send_sem.at[peer],
            recv_sem=recv_sem.at[me],
            device_id={"freq": peer},
            device_id_type=MESH,
        )

    def incoming(peer):
        return pltpu.make_async_remote_copy(
            src_ref=packed.at[peer],
            dst_ref=bins.at[peer + HALF],
            send_sem=send_sem.at[peer],
            recv_sem=recv_sem.at[peer],
            device_id={"freq": peer},
            device_id_type=MESH,
        )

    own = pltpu.make_async_copy(packed.at[me], bins.at[me + HALF], recv_sem.at[me])

    def send(i):
        tile = tile_of(i)
        for j in range(per_tile):
            peer = tile * per_tile + j

            @pl.when(peer != me)
            def _():
                outgoing(peer).start()

            @pl.when(peer == me)
            def _():
                own.start()

    def step(i, carry):
        compute(i)

        @pl.when(i == 1)
        def _():
            pl.semaphore_wait(barrier, groups + 1)

        @pl.when(i >= 1)
        def _():
            send(i - 1)

        return carry

    lax.fori_loop(0, tiles, step, 0)
    send(tiles - 1)

    def arrive(peer):
        @pl.when(peer != me)
        def _():
            incoming(peer).wait_recv()

        @pl.when(peer == me)
        def _():
            own.wait()

    def edge(which, source, target, device):
        return pltpu.make_async_remote_copy(
            src_ref=bins.at[pl.ds(source, HALF)],
            dst_ref=bins.at[pl.ds(target, HALF)],
            send_sem=edge_send.at[which],
            recv_sem=edge_recv.at[which],
            device_id={"lst": device},
            device_id_type=MESH,
        )

    to_before = edge(0, HALF, HALF + groups, before)
    to_after = edge(1, groups, 0, after)
    for peer in range(HALF):
        arrive(peer)
    to_before.start()
    for peer in range(groups - HALF, groups):
        arrive(peer)
    to_after.start()

    def arrive_loop(peer, carry):
        arrive(peer)
        return carry

    lax.fori_loop(HALF, groups - HALF, arrive_loop, 0)

    def smooth(t, carry=0):
        for part in range(2):
            total = kernel_ref[0] * bins[t, part].astype(jnp.float32)
            for shift in range(1, 2 * HALF + 1):
                total = total + kernel_ref[shift] * bins[t + shift, part].astype(jnp.float32)
            out_ref[part, t] = total.astype(jnp.bfloat16)
        return carry

    lax.fori_loop(HALF, groups - HALF, smooth, 0)
    to_before.wait_recv()
    to_after.wait_recv()
    for t in (*range(HALF), *range(groups - HALF, groups)):
        smooth(t)

    def sent(peer, carry):
        @pl.when(peer != me)
        def _():
            outgoing(peer).wait_send()

        return carry

    lax.fori_loop(0, groups, sent, 0)
    to_before.wait_send()
    to_after.wait_send()


def body(groups, blocks, visibilities, model_vis, antenna_gains, baseline_antenna_index, flag_tiles, kernel):
    count, channels = visibilities.shape[2:]
    antennas = antenna_gains.shape[2]
    tiles = channels // LANES
    width = channels // groups
    small = jnp.concatenate([baseline_antenna_index, flag_tiles[0].T]).astype(jnp.bfloat16)
    anywhere = pl.BlockSpec(memory_space=pl.ANY)
    smoothed = pl.pallas_call(
        functools.partial(gradient_kernel, groups, blocks),
        out_shape=jax.ShapeDtypeStruct((2, groups, width, antennas), jnp.bfloat16),
        in_specs=[
            anywhere,
            anywhere,
            anywhere,
            pl.BlockSpec(memory_space=pltpu.VMEM),
            pl.BlockSpec(memory_space=pltpu.SMEM),
        ],
        out_specs=pl.BlockSpec(memory_space=pltpu.VMEM),
        scratch_shapes=[
            pltpu.VMEM((tiles, 2, count, LANES), jnp.bfloat16),
            pltpu.VMEM((tiles, 2, count, LANES), jnp.bfloat16),
            pltpu.VMEM((tiles, antennas, 2 * LANES), jnp.bfloat16),
            pltpu.VMEM((2 * count, antennas), jnp.bfloat16),
            pltpu.VMEM((small.shape[0], antennas), jnp.float32),
            pltpu.VMEM((count, LANES), jnp.float32),
            pltpu.VMEM((2 * count, 2 * LANES), jnp.float32),
            pltpu.VMEM((2 * count, 2 * LANES), jnp.bfloat16),
            pltpu.VMEM((groups, 2, width, antennas), jnp.bfloat16),
            pltpu.VMEM((groups + 2 * HALF, 2, width, antennas), jnp.bfloat16),
            pltpu.SemaphoreType.DMA((tiles, 4)),
            pltpu.SemaphoreType.DMA((groups,)),
            pltpu.SemaphoreType.DMA((groups,)),
            pltpu.SemaphoreType.DMA((2,)),
            pltpu.SemaphoreType.DMA((2,)),
        ],
        compiler_params=pltpu.CompilerParams(collective_id=0, has_side_effects=True),
        name="gradient",
    )(visibilities, model_vis, antenna_gains, small, kernel)
    return jnp.swapaxes(smoothed, 2, 3)


def solution(mesh):
    in_specs = (
        P(None, ("lst", "freq"), None, None),
        P(None, ("lst", "freq"), None, None),
        P(None, ("lst", "freq"), None, None),
        P(),
        P(("lst", "freq"), None, None),
        P(),
    )
    out_specs = P(None, "lst", None, "freq")
    return jax.shard_map(
        functools.partial(body, mesh.shape["freq"], mesh.shape["lst"]),
        mesh=mesh,
        in_specs=in_specs,
        out_specs=out_specs,
        check_vma=False,
    )
```

```python
import functools

import jax
import jax.numpy as jnp
from jax import lax
from jax.experimental import pallas as pl
from jax.experimental.pallas import tpu as pltpu
from jax.sharding import PartitionSpec as P

MESH = pl.DeviceIdType.MESH
LANES = 128
ROWS = 32
HALF = 2


def over_first(left, right):
    return lax.dot_general(
        left, right, (((0,), (0,)), ((), ())), preferred_element_type=jnp.float32
    )


def gradient_kernel(
    groups,
    blocks,
    vis_ref,
    model_ref,
    gain_ref,
    index_ref,
    flag_ref,
    bins,
    data,
    model,
    gain,
    hot,
    inverse,
    weight,
    picked,
    terms,
    packed,
    stack,
    in_sem,
    send_sem,
    recv_sem,
    edge_send,
    edge_recv,
):
    tiles = data.shape[0]
    per_tile = groups // tiles
    width = LANES // per_tile
    count = data.shape[2]
    antennas = gain.shape[1]
    me = lax.axis_index("freq")
    block = lax.axis_index("lst")
    after = lax.rem(block + 1, blocks)
    before = lax.rem(block + blocks - 1, blocks)

    barrier = pltpu.get_barrier_semaphore()

    def greet(step, carry):
        peer = lax.rem(me + step, groups)
        pl.semaphore_signal(barrier, inc=1, device_id={"freq": peer}, device_id_type=MESH)
        return carry

    for peer in (before, after):
        pl.semaphore_signal(barrier, inc=1, device_id={"lst": peer}, device_id_type=MESH)
    lax.fori_loop(1, groups, greet, 0)

    def tile_of(i):
        turn = (1 - 2 * lax.rem(i, 2)) * ((i + 1) // 2)
        first = jnp.where((me < HALF) | (me >= groups - HALF), 0, tiles // 2)
        return lax.rem(me // per_tile + first + turn + tiles, tiles)

    def loads(i):
        lanes = pl.ds(pl.multiple_of(tile_of(i) * LANES, LANES), LANES)
        return [
            pltpu.make_async_copy(gain_ref.at[0, 0, :, lanes], gain.at[i, :, pl.ds(0, LANES)], in_sem.at[i, 0]),
            pltpu.make_async_copy(gain_ref.at[1, 0, :, lanes], gain.at[i, :, pl.ds(LANES, LANES)], in_sem.at[i, 1]),
            pltpu.make_async_copy(vis_ref.at[:, 0, :, lanes], data.at[i], in_sem.at[i, 2]),
            pltpu.make_async_copy(model_ref.at[:, 0, :, lanes], model.at[i], in_sem.at[i, 3]),
        ]

    def start_loads(i, carry):
        for copy in loads(i):
            copy.start()
        return carry

    lax.fori_loop(0, tiles, start_loads, 0)

    stack[0:2, :] = index_ref[...].astype(jnp.float32)
    for k in range(tiles):
        stack[k + 2 : k + 3, :] = flag_ref[k].astype(jnp.float32)
    small = stack[...].astype(jnp.bfloat16)
    row = lax.broadcasted_iota(jnp.int32, (small.shape[0], antennas), 0)
    antenna = lax.broadcasted_iota(jnp.int32, (count, antennas), 1).astype(jnp.float32)
    for which in range(2):
        label = over_first(small, (row == which).astype(jnp.bfloat16))
        hot[which * count : (which + 1) * count, :] = (label == antenna).astype(jnp.bfloat16)
    used = jnp.dot(
        small, hot[:count, :] + hot[count:, :], preferred_element_type=jnp.float32
    )
    inverse[...] = 1.0 / (1.0 + used)

    def compute(i):
        tile = tile_of(i)
        for copy in loads(i):
            copy.wait()
        picked[...] = jnp.dot(hot[...], gain[i], preferred_element_type=jnp.float32)
        weight[...] = over_first(small, (row[:, :LANES] == tile + 2).astype(jnp.bfloat16))
        for start in range(0, count, ROWS):
            here = slice(start, start + ROWS)
            there = slice(count + start, count + start + ROWS)
            first_re, first_im = picked[here, :LANES], picked[here, LANES:]
            second_re, second_im = picked[there, :LANES], picked[there, LANES:]
            data_re = data[i, 0, here, :].astype(jnp.float32)
            data_im = data[i, 1, here, :].astype(jnp.float32)
            model_re = model[i, 0, here, :].astype(jnp.float32)
            model_im = model[i, 1, here, :].astype(jnp.float32)
            flag = weight[here, :]
            cross_re = first_re * second_re + first_im * second_im
            cross_im = first_im * second_re - first_re * second_im
            pred_re = cross_re * model_re - cross_im * model_im
            pred_im = cross_re * model_im + cross_im * model_re
            resid_re = flag * (data_re - pred_re)
            resid_im = flag * (data_im - pred_im)
            along_re = second_re * model_re + second_im * model_im
            along_im = second_im * model_re - second_re * model_im
            terms[here, :LANES] = (resid_re * along_re - resid_im * along_im).astype(jnp.bfloat16)
            terms[here, LANES:] = (resid_re * along_im + resid_im * along_re).astype(jnp.bfloat16)
            other_re = first_re * model_re - first_im * model_im
            other_im = first_re * model_im + first_im * model_re
            terms[there, :LANES] = (resid_re * other_re + resid_im * other_im).astype(jnp.bfloat16)
            terms[there, LANES:] = (resid_re * other_im - resid_im * other_re).astype(jnp.bfloat16)
        sums = over_first(terms[...], hot[...])
        value = (sums * inverse[pl.ds(tile + 2, 1), :]).astype(jnp.bfloat16)
        for part in range(2):
            for j in range(per_tile):
                low = part * LANES + j * width
                packed[tile * per_tile + j, part] = value[low : low + width, :]

    def outgoing(peer):
        return pltpu.make_async_remote_copy(
            src_ref=packed.at[peer],
            dst_ref=bins.at[me + HALF],
            send_sem=send_sem.at[peer],
            recv_sem=recv_sem.at[me],
            device_id={"freq": peer},
            device_id_type=MESH,
        )

    def incoming(peer):
        return pltpu.make_async_remote_copy(
            src_ref=packed.at[peer],
            dst_ref=bins.at[peer + HALF],
            send_sem=send_sem.at[peer],
            recv_sem=recv_sem.at[peer],
            device_id={"freq": peer},
            device_id_type=MESH,
        )

    own = pltpu.make_async_copy(packed.at[me], bins.at[me + HALF], recv_sem.at[me])

    def send(i):
        tile = tile_of(i)
        for j in range(per_tile):
            peer = tile * per_tile + j

            @pl.when(peer != me)
            def _():
                outgoing(peer).start()

            @pl.when(peer == me)
            def _():
                own.start()

    def step(i, carry):
        compute(i)

        @pl.when(i == 1)
        def _():
            pl.semaphore_wait(barrier, groups + 1)

        @pl.when(i >= 1)
        def _():
            send(i - 1)

        return carry

    lax.fori_loop(0, tiles, step, 0)
    send(tiles - 1)

    def arrive(peer):
        @pl.when(peer != me)
        def _():
            incoming(peer).wait_recv()

        @pl.when(peer == me)
        def _():
            own.wait()

    def edge(which):
        forward = which < HALF
        source = HALF + which if forward else groups + which - HALF
        return pltpu.make_async_remote_copy(
            src_ref=bins.at[source],
            dst_ref=bins.at[source + groups if forward else source - groups],
            send_sem=edge_send.at[which],
            recv_sem=edge_recv.at[which],
            device_id={"lst": before if forward else after},
            device_id_type=MESH,
        )

    for which in range(2 * HALF):
        arrive(which if which < HALF else groups + which - 2 * HALF)
        edge(which).start()

    def arrive_loop(peer, carry):
        arrive(peer)
        return carry

    lax.fori_loop(HALF, groups - HALF, arrive_loop, 0)

    for which in range(2 * HALF):
        edge(which).wait_recv()
    def sent(peer, carry):
        @pl.when(peer != me)
        def _():
            outgoing(peer).wait_send()

        return carry

    lax.fori_loop(0, groups, sent, 0)
    for which in range(2 * HALF):
        edge(which).wait_send()


def smooth_kernel(kernel_ref, bins_ref, out_ref):
    def smooth(t, carry):
        total = kernel_ref[0] * bins_ref[t, 0].astype(jnp.float32)
        for shift in range(1, 2 * HALF + 1):
            total = total + kernel_ref[shift] * bins_ref[t + shift, 0].astype(jnp.float32)
        out_ref[0, t] = total.astype(jnp.bfloat16)
        return carry

    lax.fori_loop(0, out_ref.shape[1], smooth, 0)


def body(groups, blocks, visibilities, model_vis, antenna_gains, baseline_antenna_index, flag_tiles, kernel):
    count, channels = visibilities.shape[2:]
    antennas = antenna_gains.shape[2]
    tiles = channels // LANES
    width = channels // groups
    rows = tiles + 2
    held = groups + 2 * HALF
    anywhere = pl.BlockSpec(memory_space=pl.ANY)
    in_vmem = pl.BlockSpec(memory_space=pltpu.VMEM)
    bins = pl.pallas_call(
        functools.partial(gradient_kernel, groups, blocks),
        out_shape=jax.ShapeDtypeStruct((held, 2, width, antennas), jnp.bfloat16),
        in_specs=[anywhere, anywhere, anywhere, in_vmem, in_vmem],
        out_specs=anywhere,
        scratch_shapes=[
            pltpu.VMEM((tiles, 2, count, LANES), jnp.bfloat16),
            pltpu.VMEM((tiles, 2, count, LANES), jnp.bfloat16),
            pltpu.VMEM((tiles, antennas, 2 * LANES), jnp.bfloat16),
            pltpu.VMEM((2 * count, antennas), jnp.bfloat16),
            pltpu.VMEM((rows, antennas), jnp.float32),
            pltpu.VMEM((count, LANES), jnp.float32),
            pltpu.VMEM((2 * count, 2 * LANES), jnp.float32),
            pltpu.VMEM((2 * count, 2 * LANES), jnp.bfloat16),
            pltpu.VMEM((groups, 2, width, antennas), jnp.bfloat16),
            pltpu.VMEM((rows, count), jnp.float32),
            pltpu.SemaphoreType.DMA((tiles, 4)),
            pltpu.SemaphoreType.DMA((groups,)),
            pltpu.SemaphoreType.DMA((groups,)),
            pltpu.SemaphoreType.DMA((2 * HALF,)),
            pltpu.SemaphoreType.DMA((2 * HALF,)),
        ],
        compiler_params=pltpu.CompilerParams(collective_id=0, has_side_effects=True),
        name="gradient",
    )(
        visibilities,
        model_vis,
        antenna_gains,
        baseline_antenna_index,
        jnp.transpose(flag_tiles, (2, 0, 1)),
    )
    smoothed = pl.pallas_call(
        smooth_kernel,
        out_shape=jax.ShapeDtypeStruct((2, groups, width, antennas), jnp.bfloat16),
        grid=(2,),
        in_specs=[
            pl.BlockSpec(memory_space=pltpu.SMEM),
            pl.BlockSpec((held, 1, width, antennas), lambda part: (0, part, 0, 0)),
        ],
        out_specs=pl.BlockSpec((1, groups, width, antennas), lambda part: (part, 0, 0, 0)),
        name="smooth",
    )(kernel, bins)
    return jnp.swapaxes(smoothed, 2, 3)


def solution(mesh):
    in_specs = (
        P(None, ("lst", "freq"), None, None),
        P(None, ("lst", "freq"), None, None),
        P(None, ("lst", "freq"), None, None),
        P(),
        P(("lst", "freq"), None, None),
        P(),
    )
    out_specs = P(None, "lst", None, "freq")
    return jax.shard_map(
        functools.partial(body, mesh.shape["freq"], mesh.shape["lst"]),
        mesh=mesh,
        in_specs=in_specs,
        out_specs=out_specs,
        check_vma=False,
    )
```

```python
import functools

import jax
import jax.numpy as jnp
from jax import lax
from jax.experimental import pallas as pl
from jax.experimental.pallas import tpu as pltpu
from jax.sharding import PartitionSpec as P

MESH = pl.DeviceIdType.MESH
LANES = 128
ROWS = 32
HALF = 2


def over_first(left, right):
    return lax.dot_general(
        left, right, (((0,), (0,)), ((), ())), preferred_element_type=jnp.float32
    )


def gradient_kernel(
    groups,
    blocks,
    vis_ref,
    model_ref,
    gain_ref,
    index_ref,
    flag_ref,
    bins,
    data,
    model,
    gain,
    hot,
    inverse,
    weight,
    picked,
    terms,
    packed,
    stack,
    in_sem,
    send_sem,
    recv_sem,
    edge_send,
    edge_recv,
):
    tiles = data.shape[0]
    per_tile = groups // tiles
    width = LANES // per_tile
    count = data.shape[2]
    antennas = gain.shape[1]
    me = lax.axis_index("freq")
    block = lax.axis_index("lst")
    after = lax.rem(block + 1, blocks)
    before = lax.rem(block + blocks - 1, blocks)

    barrier = pltpu.get_barrier_semaphore()

    def greet(step, carry):
        peer = lax.rem(me + step, groups)
        pl.semaphore_signal(barrier, inc=1, device_id={"freq": peer}, device_id_type=MESH)
        return carry

    for peer in (before, after):
        pl.semaphore_signal(barrier, inc=1, device_id={"lst": peer}, device_id_type=MESH)
    lax.fori_loop(1, groups, greet, 0)

    def tile_of(i):
        turn = (1 - 2 * lax.rem(i, 2)) * ((i + 1) // 2)
        first = jnp.where((me < HALF) | (me >= groups - HALF), 0, tiles // 2)
        return lax.rem(me // per_tile + first + turn + tiles, tiles)

    def loads(i):
        lanes = pl.ds(pl.multiple_of(tile_of(i) * LANES, LANES), LANES)
        return [
            pltpu.make_async_copy(gain_ref.at[0, 0, :, lanes], gain.at[i, :, pl.ds(0, LANES)], in_sem.at[i, 0]),
            pltpu.make_async_copy(gain_ref.at[1, 0, :, lanes], gain.at[i, :, pl.ds(LANES, LANES)], in_sem.at[i, 1]),
            pltpu.make_async_copy(vis_ref.at[:, 0, :, lanes], data.at[i], in_sem.at[i, 2]),
            pltpu.make_async_copy(model_ref.at[:, 0, :, lanes], model.at[i], in_sem.at[i, 3]),
        ]

    def start_loads(i, carry):
        for copy in loads(i):
            copy.start()
        return carry

    lax.fori_loop(0, tiles, start_loads, 0)

    stack[0:2, :] = index_ref[...].astype(jnp.float32)
    for k in range(tiles):
        stack[k + 2 : k + 3, :] = flag_ref[k].astype(jnp.float32)
    small = stack[...].astype(jnp.bfloat16)
    row = lax.broadcasted_iota(jnp.int32, (small.shape[0], antennas), 0)
    antenna = lax.broadcasted_iota(jnp.int32, (count, antennas), 1).astype(jnp.float32)
    for which in range(2):
        label = over_first(small, (row == which).astype(jnp.bfloat16))
        hot[which * count : (which + 1) * count, :] = (label == antenna).astype(jnp.bfloat16)
    used = jnp.dot(
        small, hot[:count, :] + hot[count:, :], preferred_element_type=jnp.float32
    )
    inverse[...] = 1.0 / (1.0 + used)

    def compute(i):
        tile = tile_of(i)
        for copy in loads(i):
            copy.wait()
        picked[...] = jnp.dot(hot[...], gain[i], preferred_element_type=jnp.float32)
        weight[...] = over_first(small, (row[:, :LANES] == tile + 2).astype(jnp.bfloat16))
        for start in range(0, count, ROWS):
            here = slice(start, start + ROWS)
            there = slice(count + start, count + start + ROWS)
            first_re, first_im = picked[here, :LANES], picked[here, LANES:]
            second_re, second_im = picked[there, :LANES], picked[there, LANES:]
            data_re = data[i, 0, here, :].astype(jnp.float32)
            data_im = data[i, 1, here, :].astype(jnp.float32)
            model_re = model[i, 0, here, :].astype(jnp.float32)
            model_im = model[i, 1, here, :].astype(jnp.float32)
            flag = weight[here, :]
            cross_re = first_re * second_re + first_im * second_im
            cross_im = first_im * second_re - first_re * second_im
            pred_re = cross_re * model_re - cross_im * model_im
            pred_im = cross_re * model_im + cross_im * model_re
            resid_re = flag * (data_re - pred_re)
            resid_im = flag * (data_im - pred_im)
            along_re = second_re * model_re + second_im * model_im
            along_im = second_im * model_re - second_re * model_im
            terms[here, :LANES] = (resid_re * along_re - resid_im * along_im).astype(jnp.bfloat16)
            terms[here, LANES:] = (resid_re * along_im + resid_im * along_re).astype(jnp.bfloat16)
            other_re = first_re * model_re - first_im * model_im
            other_im = first_re * model_im + first_im * model_re
            terms[there, :LANES] = (resid_re * other_re + resid_im * other_im).astype(jnp.bfloat16)
            terms[there, LANES:] = (resid_re * other_im - resid_im * other_re).astype(jnp.bfloat16)
        sums = over_first(terms[...], hot[...])
        value = (sums * inverse[pl.ds(tile + 2, 1), :]).astype(jnp.bfloat16)
        for part in range(2):
            for j in range(per_tile):
                low = part * LANES + j * width
                packed[tile * per_tile + j, part] = value[low : low + width, :]

    def outgoing(peer):
        return pltpu.make_async_remote_copy(
            src_ref=packed.at[peer],
            dst_ref=bins.at[me + HALF],
            send_sem=send_sem.at[peer],
            recv_sem=recv_sem.at[me],
            device_id={"freq": peer},
            device_id_type=MESH,
        )

    def incoming(peer):
        return pltpu.make_async_remote_copy(
            src_ref=packed.at[peer],
            dst_ref=bins.at[peer + HALF],
            send_sem=send_sem.at[peer],
            recv_sem=recv_sem.at[peer],
            device_id={"freq": peer},
            device_id_type=MESH,
        )

    own = pltpu.make_async_copy(packed.at[me], bins.at[me + HALF], recv_sem.at[me])

    def send(i):
        tile = tile_of(i)
        for j in range(per_tile):
            peer = tile * per_tile + j

            @pl.when(peer != me)
            def _():
                outgoing(peer).start()

            @pl.when(peer == me)
            def _():
                own.start()

    def step(i, carry):
        compute(i)

        @pl.when(i == 0)
        def _():
            pl.semaphore_wait(barrier, groups + 1)

        send(i)
        return carry

    lax.fori_loop(0, tiles, step, 0)

    def arrive(peer):
        @pl.when(peer != me)
        def _():
            incoming(peer).wait_recv()

        @pl.when(peer == me)
        def _():
            own.wait()

    def edge(which):
        forward = which < HALF
        source = HALF + which if forward else groups + which - HALF
        return pltpu.make_async_remote_copy(
            src_ref=bins.at[source],
            dst_ref=bins.at[source + groups if forward else source - groups],
            send_sem=edge_send.at[which],
            recv_sem=edge_recv.at[which],
            device_id={"lst": before if forward else after},
            device_id_type=MESH,
        )

    for which in range(2 * HALF):
        arrive(which if which < HALF else groups + which - 2 * HALF)
        edge(which).start()

    def arrive_loop(peer, carry):
        arrive(peer)
        return carry

    lax.fori_loop(HALF, groups - HALF, arrive_loop, 0)

    for which in range(2 * HALF):
        edge(which).wait_recv()
    def sent(peer, carry):
        @pl.when(peer != me)
        def _():
            outgoing(peer).wait_send()

        return carry

    lax.fori_loop(0, groups, sent, 0)
    for which in range(2 * HALF):
        edge(which).wait_send()


def smooth_kernel(kernel_ref, bins_ref, out_ref, done, out_sem):
    pieces, times, rows = done.shape[:3]
    per_part = pieces // 2

    def place(piece):
        return piece // per_part, pl.ds(piece % per_part * rows, rows)

    def store(piece):
        part, here = place(piece)
        return pltpu.make_async_copy(done.at[piece], out_ref.at[part, :, here], out_sem.at[piece])

    taps = [kernel_ref[shift] for shift in range(2 * HALF + 1)]

    def smooth(piece):
        part, here = place(piece)
        window = [bins_ref[t, part, here].astype(jnp.float32) for t in range(2 * HALF)]
        for t in range(times):
            window.append(bins_ref[t + 2 * HALF, part, here].astype(jnp.float32))
            total = taps[0] * window[0]
            for tap, value in zip(taps[1:], window[1:]):
                total = total + tap * value
            done[piece, t] = total.astype(jnp.bfloat16)
            window.pop(0)

    for piece in range(pieces):
        smooth(piece)
        store(piece).start()
    for piece in range(pieces):
        store(piece).wait()


def body(groups, blocks, visibilities, model_vis, antenna_gains, baseline_antenna_index, flag_tiles, kernel):
    count, channels = visibilities.shape[2:]
    antennas = antenna_gains.shape[2]
    tiles = channels // LANES
    width = channels // groups
    rows = tiles + 2
    held = groups + 2 * HALF
    anywhere = pl.BlockSpec(memory_space=pl.ANY)
    in_vmem = pl.BlockSpec(memory_space=pltpu.VMEM)
    bins = pl.pallas_call(
        functools.partial(gradient_kernel, groups, blocks),
        out_shape=pltpu.VMEM((held, 2, width, antennas), jnp.bfloat16),
        in_specs=[anywhere, anywhere, anywhere, in_vmem, in_vmem],
        out_specs=in_vmem,
        scratch_shapes=[
            pltpu.VMEM((tiles, 2, count, LANES), jnp.bfloat16),
            pltpu.VMEM((tiles, 2, count, LANES), jnp.bfloat16),
            pltpu.VMEM((tiles, antennas, 2 * LANES), jnp.bfloat16),
            pltpu.VMEM((2 * count, antennas), jnp.bfloat16),
            pltpu.VMEM((rows, antennas), jnp.float32),
            pltpu.VMEM((count, LANES), jnp.float32),
            pltpu.VMEM((2 * count, 2 * LANES), jnp.float32),
            pltpu.VMEM((2 * count, 2 * LANES), jnp.bfloat16),
            pltpu.VMEM((groups, 2, width, antennas), jnp.bfloat16),
            pltpu.VMEM((rows, count), jnp.float32),
            pltpu.SemaphoreType.DMA((tiles, 4)),
            pltpu.SemaphoreType.DMA((groups,)),
            pltpu.SemaphoreType.DMA((groups,)),
            pltpu.SemaphoreType.DMA((2 * HALF,)),
            pltpu.SemaphoreType.DMA((2 * HALF,)),
        ],
        compiler_params=pltpu.CompilerParams(collective_id=0, has_side_effects=True),
        name="gradient",
    )(
        visibilities,
        model_vis,
        antenna_gains,
        baseline_antenna_index,
        jnp.transpose(flag_tiles, (2, 0, 1)),
    )
    bins = pltpu.with_memory_space_constraint(bins, pltpu.VMEM)
    smoothed = pl.pallas_call(
        smooth_kernel,
        out_shape=jax.ShapeDtypeStruct((2, groups, width, antennas), jnp.bfloat16),
        in_specs=[pl.BlockSpec(memory_space=pltpu.SMEM), in_vmem],
        out_specs=anywhere,
        scratch_shapes=[
            pltpu.VMEM((4, groups, width // 2, antennas), jnp.bfloat16),
            pltpu.SemaphoreType.DMA((4,)),
        ],
        name="smooth",
    )(kernel, bins)
    return jnp.swapaxes(smoothed, 2, 3)


def solution(mesh):
    in_specs = (
        P(None, ("lst", "freq"), None, None),
        P(None, ("lst", "freq"), None, None),
        P(None, ("lst", "freq"), None, None),
        P(),
        P(("lst", "freq"), None, None),
        P(),
    )
    out_specs = P(None, "lst", None, "freq")
    return jax.shard_map(
        functools.partial(body, mesh.shape["freq"], mesh.shape["lst"]),
        mesh=mesh,
        in_specs=in_specs,
        out_specs=out_specs,
        check_vma=False,
    )
```
